32 devices in a mesh: frame: 4 (over y, x), sector: 8 (over z, core).
Axes of the slice: x: 2, y: 2, z: 4, core: 2. Of those that a mesh axis runs over, the one named last changes fastest.
Arguments:
- camera: bfloat16 [4096, 1536], P(('frame', 'sector')), may hold values from -6 to 6
- owners: int32 [256], P(('frame', 'sector')), may hold values from 0 to 7, as said below
- unit_slots: int32 [256, 8], P(('frame', 'sector')), may hold values from 0 to 15, as said below
- pool_weights: bfloat16 [256, 8, 16, 128], P(('frame', 'sector')), may hold values from -0.0234375 to 0.0234375
- student: bfloat16 [32768, 512], P(('frame', 'sector')), may hold values from -0.25 to 0.25
- head_weight: bfloat16 [1536, 512], replicated, may hold values from -0.15625 to 0.15625
Outputs:
- grad_student: bfloat16 [32768, 512], P(('frame', 'sector'))
- grad_head: float32 [1536, 512], P('sector')
The draws below stay inside these ranges and needn't reach their ends.
Inputs may be any that keep to these rules, and one draw needn't show every extreme that they name: `owners`: in every frame group a device sends at most 2 of its units to any one sector, one sector receives exactly 2 units from every device of the group, and every sector receives at least one unit. `unit_slots`: an entry q of a lidar block held by sector o of frame group f names the unit of rank q % 2 among the units of device q // 2 of group f that are owned by o; that unit exists, and every unit is named by at least one entry of its owner.
All inputs are finite; a program needn't handle non-finite values.
Results may differ from the reference program's by a relative error of at most 0.005.
Values may be sent and summed in bfloat16 or wider, within the bound.
A program may use at most 64 MiB of HBM per device.

```python
import jax
import jax.numpy as jnp
from jax import lax

C = 1536
HD = 512
UNIT = 16
LBR = 128
KREF = 8
CAP = 2
LB_DEV = 8
U_DEV = 8
CAMROWS = 4096
LBLOCKS = 256
LIDTOK = 32768
N_FRAME = 4
N_SECTOR = 8


def routing(key):

    def one_group(group_key):
        busy_key, senders_key, slots_key = jax.random.split(group_key, 3)
        busiest = jax.random.randint(busy_key, (), 0, N_SECTOR).astype(jnp.int32)

        def one_sender(sender, sender_key):
            score_key, order_key = jax.random.split(sender_key)
            slot_count = CAP * (N_SECTOR - 1)
            scores = jax.random.permutation(score_key, slot_count).astype(jnp.int32)
            forced = CAP * (sender % (N_SECTOR - 1))
            scores = jnp.where(jnp.arange(slot_count) == forced, slot_count, scores)
            top_values, picked = lax.top_k(scores, U_DEV - CAP)
            others = (picked // CAP).astype(jnp.int32)
            targets = jnp.where(others < busiest, others, others + 1)
            listed = jnp.concatenate([jnp.full((CAP,), 1, jnp.int32) * busiest, targets])
            return jax.random.permutation(order_key, listed)
        owner_table = jax.vmap(one_sender)(jnp.arange(N_SECTOR, dtype=jnp.int32), jax.random.split(senders_key, N_SECTOR))
        counts = jnp.sum((owner_table[:, :, None] == jnp.arange(N_SECTOR)[None, None, :]).astype(jnp.int32), axis=1)

        def one_owner(owner_index, owner_key):
            slot_ids = jnp.arange(N_SECTOR * CAP, dtype=jnp.int32)
            filled = slot_ids % CAP < counts[slot_ids // CAP, owner_index]
            ordered = jnp.sort(jnp.where(filled, slot_ids, N_SECTOR * CAP + slot_ids))
            live_slots = jnp.sum(filled.astype(jnp.int32))
            chosen = jax.random.permutation(owner_key, LB_DEV * KREF).astype(jnp.int32) % live_slots
            return ordered[chosen]
        slot_table = jax.vmap(one_owner)(jnp.arange(N_SECTOR, dtype=jnp.int32), jax.random.split(slots_key, N_SECTOR))
        return (owner_table, slot_table)
    return jax.vmap(one_group)(jax.random.split(key, N_FRAME))


def draw_owners(key, part):
    owner_table, slot_table = routing(jax.random.fold_in(key, 7))
    return owner_table.reshape(-1).astype(jnp.int32)


def draw_unit_slots(key, part):
    owner_table, slot_table = routing(jax.random.fold_in(key, 7))
    return slot_table.reshape(-1, KREF).astype(jnp.int32)


def level_of(stream_key, dims, shards, least, high):
    gain = 1.0
    for position, parts in shards:
        heights = jax.random.uniform(jax.random.fold_in(jax.random.fold_in(stream_key, 6), position), (parts,), jnp.float32, least / len(shards), high / len(shards))
        gain = gain * jnp.repeat(jnp.exp(heights), dims[position] // parts).reshape((-1,) + (1,) * (len(dims) - 1 - position))
    return gain


def scatter_about(stream_key, shape, width, reach, cuts=(), kind=jnp.bfloat16):
    values = width * jax.random.normal(stream_key, shape, jnp.float32)
    if cuts:
        values = values * level_of(stream_key, shape, cuts, -0.22, 0.18)
    return jnp.clip(values, -reach, reach).astype(kind)


def setup_inputs(seed: int = 0) -> dict:
    arg_keys = jax.random.split(jax.random.key(seed), 7)
    return {
        "camera": scatter_about(arg_keys[0], (CAMROWS, C), 1.0, 6.0, ((0, 32),)),
        "owners": draw_owners(jax.random.fold_in(arg_keys[6], 71), 0),
        "unit_slots": draw_unit_slots(jax.random.fold_in(arg_keys[6], 71), 0),
        "pool_weights": scatter_about(arg_keys[3], (LBLOCKS, KREF, UNIT, LBR), (KREF * UNIT * HD) ** -0.5, 0.0234375, ((0, 32),)),
        "student": scatter_about(arg_keys[4], (LIDTOK, HD), HD ** -0.5, 0.25, ((0, 32),)),
        "head_weight": scatter_about(arg_keys[5], (C, HD), C ** -0.5, 0.15625),
    }


LOSS_WEIGHT = 8.0
EPSILON = 1e-06

def cosine_grads(target, student):
    learner = student.astype(jnp.float32)
    norm_teacher = jnp.sqrt(lax.optimization_barrier(jnp.sum(target * target, axis=-1, keepdims=True)) + EPSILON)
    norm_learner = jnp.sqrt(lax.optimization_barrier(jnp.sum(learner * learner, axis=-1, keepdims=True)) + EPSILON)
    cosine = lax.optimization_barrier(jnp.sum(target * learner, axis=-1, keepdims=True)) / (norm_teacher * norm_learner)
    grad_learner = -LOSS_WEIGHT * (target / (norm_teacher * norm_learner) - cosine * learner / (norm_learner * norm_learner))
    grad_teacher = -LOSS_WEIGHT * (learner / (norm_teacher * norm_learner) - cosine * target / (norm_teacher * norm_teacher))
    return (grad_teacher.astype(jnp.bfloat16), grad_learner.astype(jnp.bfloat16))

def ranks_of(owner_table):
    count_units = owner_table.shape[1]
    earlier = jnp.arange(count_units)[:, None] > jnp.arange(count_units)[None, :]
    matching = owner_table[:, :, None] == owner_table[:, None, :]
    return lax.optimization_barrier(jnp.sum(jnp.where(earlier[None] & matching, 1, 0), axis=2)).astype(jnp.int32)

def reference(camera, owners, unit_slots, pool_weights, student, head_weight):
    sectors = N_SECTOR
    camera_groups = camera.reshape(N_FRAME, sectors * U_DEV, UNIT, C)
    owner_groups = owners.reshape(N_FRAME, sectors, U_DEV)
    slot_groups = unit_slots.reshape(N_FRAME, sectors, LB_DEV * KREF)
    weight_groups = pool_weights.reshape(N_FRAME, sectors * LB_DEV, KREF, UNIT, LBR)
    student_groups = student.reshape(N_FRAME, sectors * LB_DEV * LBR, HD)

    def one_group(running, inputs):
        camera_group, owner_group, slot_group, weight_group, student_group = inputs
        rank_group = ranks_of(owner_group)
        senders = jnp.arange(sectors, dtype=jnp.int32)[:, None]
        keys = owner_group * (sectors * CAP) + senders * CAP + rank_group
        table = jnp.zeros((sectors * sectors * CAP,), jnp.int32).at[keys.reshape(-1)].set(jnp.arange(sectors * U_DEV, dtype=jnp.int32))
        owner_ids = jnp.arange(sectors, dtype=jnp.int32)[:, None]
        source = table[(owner_ids * (sectors * CAP) + slot_group).reshape(-1)]
        flat_camera = camera_group.reshape(-1, C)
        projected = jnp.dot(flat_camera, head_weight, preferred_element_type=jnp.float32).astype(jnp.bfloat16)
        projected = projected.reshape(sectors * U_DEV, UNIT, HD)
        chosen = projected[source].reshape(sectors * LB_DEV, KREF, UNIT, HD)
        weights_wide = weight_group.astype(jnp.float32)
        target = jnp.einsum('bkjl,bkjh->blh', weights_wide, chosen.astype(jnp.float32)).reshape(-1, HD)
        grad_teacher, grad_learner = cosine_grads(target, student_group)
        spread = jnp.einsum('bkjl,blh->bkjh', weights_wide, grad_teacher.reshape(-1, LBR, HD).astype(jnp.float32))
        unit_grad = jax.ops.segment_sum(spread.reshape(-1, UNIT * HD), source, num_segments=sectors * U_DEV).astype(jnp.bfloat16)
        head_term = jnp.dot(flat_camera.T, unit_grad.reshape(-1, HD), preferred_element_type=jnp.float32)
        return (running + head_term, grad_learner)
    total, learner_grads = lax.scan(one_group, jnp.zeros((C, HD), jnp.float32), (camera_groups, owner_groups, slot_groups, weight_groups, student_groups))
    return (learner_grads.reshape(-1, HD), total)
```

```python
import functools

import jax
import jax.numpy as jnp
from jax import lax
from jax.experimental import pallas as pl
from jax.experimental.pallas import tpu as pltpu
from jax.sharding import PartitionSpec as P

CAP = 2
LOSS_WEIGHT = 8.0
EPSILON = 1e-06
F32 = jnp.float32
BF16 = jnp.bfloat16


def dot(a, b):
    return jnp.dot(a, b, preferred_element_type=F32)


def kernel_body(
    sizes,
    owners,
    slots,
    cam_h,
    pool_h,
    stu_h,
    w_h,
    gs_h,
    gh,
    cam,
    pool,
    stu,
    w,
    send,
    recv,
    camt,
    camg,
    bmat,
    bt,
    gt,
    gsv,
    sg,
    back,
    gall,
    acc,
    rsend,
    rrecv,
    fgat,
    load_sem,
    store_sem,
    fs,
    fr,
    cs,
    cr,
    bs,
    br,
    gs_sem,
    gr_sem,
    ps,
    pr,
    xs,
    xr,
    ys,
    yr,
):
    n, nf, units, unit, blocks, refs, lbr, fused = sizes
    rows, width = cam.shape
    head = w.shape[1]
    slot_rows = n * CAP * unit
    part = width // n
    me = lax.axis_index("sector")
    mf = lax.axis_index("frame")

    loads = [
        pltpu.make_async_copy(src, dst, load_sem.at[i])
        for i, (src, dst) in enumerate(((cam_h, cam), (w_h, w), (pool_h, pool), (stu_h, stu)))
    ]
    for copy in loads:
        copy.start()

    def remote(src, dst, ssem, rsem, frame, sector):
        return pltpu.make_async_remote_copy(
            src_ref=src,
            dst_ref=dst,
            send_sem=ssem,
            recv_sem=rsem,
            device_id=(frame, sector),
            device_id_type=pl.DeviceIdType.MESH,
        )

    barrier = pltpu.get_barrier_semaphore()
    for i in range(1, n):
        pl.semaphore_signal(
            barrier, inc=1, device_id=(mf, lax.rem(me + i, n)), device_id_type=pl.DeviceIdType.MESH
        )
    greeted = n - 1
    if fused:
        for i in range(1, nf):
            pl.semaphore_signal(
                barrier,
                inc=1,
                device_id=(lax.rem(mf + i, nf), me),
                device_id_type=pl.DeviceIdType.MESH,
            )
        greeted += nf - 1

    dest = []
    for u in range(units):
        rank = jnp.int32(0)
        for v in range(u):
            rank = rank + jnp.where(owners[v] == owners[u], 1, 0).astype(jnp.int32)
        dest.append(owners[u] * CAP + rank)

    column = lax.broadcasted_iota(jnp.int32, (1, rows), 1)
    place_row = lax.rem(column, unit)
    for u in range(units):
        place_row = place_row + jnp.where(column // unit == u, dest[u] * unit, 0)
    place = (
        lax.broadcasted_iota(jnp.int32, (slot_rows, rows), 0) == place_row
    ).astype(F32).astype(BF16)

    loads[0].wait()
    loads[1].wait()
    projected = dot(cam[...], w[...]).astype(BF16)
    placed = dot(place, projected).astype(BF16).reshape(n, CAP * unit, head)
    send[...] = placed
    pl.semaphore_wait(barrier, greeted)
    forward = []
    for i in range(1, n):
        peer = lax.rem(me + i, n)
        copy = remote(send.at[peer], recv.at[me], fs.at[i], fr.at[i], mf, peer)
        copy.start()
        forward.append(copy)
    recv[me] = send[me]

    for i in range(0, width, 128):
        camt[i : i + 128, :] = cam[:, i : i + 128].T
    columns = []
    for i in range(1, n):
        peer = lax.rem(me + i, n)
        start = pl.multiple_of(peer * part, 16)
        copy = remote(camt.at[pl.ds(start, part)], camg.at[me], cs.at[i], cr.at[i], mf, peer)
        copy.start()
        columns.append(copy)
    camg[me] = camt[pl.ds(pl.multiple_of(me * part, 16), part), :]

    loads[2].wait()
    depth = refs * unit
    ref_column = lax.broadcasted_iota(jnp.int32, (1, depth), 1)
    slot_row = lax.broadcasted_iota(jnp.int32, (slot_rows, depth), 0)
    for b in range(blocks):
        wanted = lax.rem(ref_column, unit)
        for k in range(refs):
            wanted = wanted + jnp.where(ref_column // unit == k, slots[b, k] * unit, 0)
        pick = (slot_row == wanted).astype(F32).astype(BF16)
        combined = dot(pick, pool[b * depth : (b + 1) * depth, :])
        bmat[:, b * lbr : (b + 1) * lbr] = combined.astype(BF16)
        bt[b * lbr : (b + 1) * lbr, :] = combined.T.astype(BF16)

    loads[3].wait()
    for copy in forward:
        copy.wait_recv()
    arrived = recv[...].reshape(slot_rows, head)
    stores = []
    for b in range(blocks):
        span = slice(b * lbr, (b + 1) * lbr)
        target = dot(bt[span, :], arrived)
        learner = stu[span, :].astype(F32)
        inv_t = lax.rsqrt(jnp.sum(target * target, axis=1, keepdims=True) + EPSILON)
        inv_l = lax.rsqrt(jnp.sum(learner * learner, axis=1, keepdims=True) + EPSILON)
        both = inv_t * inv_l
        cosine = jnp.sum(target * learner, axis=1, keepdims=True) * both
        scale = -LOSS_WEIGHT * both
        back_l = LOSS_WEIGHT * cosine * (inv_l * inv_l)
        back_t = LOSS_WEIGHT * cosine * (inv_t * inv_t)
        gsv[span, :] = (target * scale + learner * back_l).astype(BF16)
        gt[span, :] = (learner * scale + target * back_t).astype(BF16)
        store = pltpu.make_async_copy(gsv.at[span], gs_h.at[span], store_sem.at[b])
        store.start()
        stores.append(store)

    sg[...] = dot(bmat[...], gt[...]).astype(BF16).reshape(n, CAP * unit, head)
    returns = []
    for i in range(1, n):
        peer = lax.rem(me + i, n)
        copy = remote(sg.at[peer], back.at[me], bs.at[i], br.at[i], mf, peer)
        copy.start()
        returns.append(copy)
    back[me] = sg[me]

    place_column = lax.broadcasted_iota(jnp.int32, (rows, 1), 0)
    home_row = lax.rem(place_column, unit)
    for u in range(units):
        home_row = home_row + jnp.where(place_column // unit == u, dest[u] * unit, 0)
    home = (
        lax.broadcasted_iota(jnp.int32, (rows, slot_rows), 1) == home_row
    ).astype(F32).astype(BF16)
    for copy in returns:
        copy.wait_recv()
    gall[me] = dot(home, back[...].reshape(slot_rows, head)).astype(BF16)

    nz = n // 2
    z = me // 2
    core = lax.rem(me, 2)
    twin = z * 2 + (1 - core)
    gathers = [None]
    for i in range(1, nz):
        peer = lax.rem(z + i, nz) * 2 + core
        copy = remote(gall.at[me], gall.at[me], gs_sem.at[i], gr_sem.at[i], mf, peer)
        copy.start()
        gathers.append(copy)
    passed = [remote(gall.at[me], gall.at[me], ps.at[0], pr.at[0], mf, twin)]
    passed[0].start()
    for copy in columns:
        copy.wait_recv()
    acc[...] = dot(camg[me], gall[me])
    for i in range(1, nz):
        source = lax.rem(z + nz - i, nz) * 2 + core
        gathers[i].wait_recv()
        copy = remote(gall.at[source], gall.at[source], ps.at[i], pr.at[i], mf, twin)
        copy.start()
        passed.append(copy)
        acc[...] += dot(camg[source], gall[source])
    for i in range(nz):
        source = lax.rem(z + nz - i, nz) * 2 + (1 - core)
        passed[i].wait_recv()
        acc[...] += dot(camg[source], gall[source])

    pending = forward + columns + returns + gathers[1:] + passed
    if fused:
        quarter = part // nf
        rsend[...] = acc[...].astype(BF16)
        sums = []
        for i in range(1, nf):
            peer = lax.rem(mf + i, nf)
            start = pl.multiple_of(peer * quarter, 16)
            copy = remote(
                rsend.at[pl.ds(start, quarter)], rrecv.at[i], xs.at[i], xr.at[i], peer, me
            )
            copy.start()
            sums.append(copy)
        total = acc[pl.ds(pl.multiple_of(mf * quarter, 16), quarter), :]
        for i in range(1, nf):
            sums[i - 1].wait_recv()
            total = total + rrecv[i].astype(F32)
        fgat[mf] = total.astype(BF16)
        spreads = []
        for i in range(1, nf):
            peer = lax.rem(mf + i, nf)
            copy = remote(fgat.at[mf], fgat.at[mf], ys.at[i], yr.at[i], peer, me)
            copy.start()
            spreads.append(copy)
        for copy in spreads:
            copy.wait_recv()
        for f in range(nf):
            gh[f * quarter : (f + 1) * quarter, :] = fgat[f].astype(F32)
        pending = pending + sums + spreads
    else:
        gh[...] = acc[...]
    for copy in pending:
        copy.wait_send()
    for store in stores:
        store.wait()


def on_device(camera, owners, unit_slots, pool_weights, student, head_weight):
    n = lax.axis_size("sector")
    nf = lax.axis_size("frame")
    units = owners.shape[0]
    rows, width = camera.shape
    unit = rows // units
    head = head_weight.shape[1]
    blocks, refs = unit_slots.shape
    lbr = pool_weights.shape[3]
    tokens = blocks * lbr
    slot_rows = n * CAP * unit
    part = width // n
    fused = part % (nf * 16) == 0
    quarter = part // nf if fused else 16
    sizes = (n, nf, units, unit, blocks, refs, lbr, fused)
    any_space = pl.BlockSpec(memory_space=pl.ANY)
    smem = pl.BlockSpec(memory_space=pltpu.SMEM)
    dma = pltpu.SemaphoreType.DMA
    grad_student, grad_head = pl.pallas_call(
        functools.partial(kernel_body, sizes),
        out_shape=(
            jax.ShapeDtypeStruct((tokens, head), BF16),
            jax.ShapeDtypeStruct((part, head), F32),
        ),
        in_specs=[smem, smem, any_space, any_space, any_space, any_space],
        out_specs=(any_space, pl.BlockSpec(memory_space=pltpu.VMEM)),
        scratch_shapes=[
            pltpu.VMEM((rows, width), BF16),
            pltpu.VMEM((blocks * refs * unit, lbr), BF16),
            pltpu.VMEM((tokens, head), BF16),
            pltpu.VMEM((width, head), BF16),
            pltpu.VMEM((n, CAP * unit, head), BF16),
            pltpu.VMEM((n, CAP * unit, head), BF16),
            pltpu.VMEM((width, rows), BF16),
            pltpu.VMEM((n, part, rows), BF16),
            pltpu.VMEM((slot_rows, tokens), BF16),
            pltpu.VMEM((tokens, slot_rows), BF16),
            pltpu.VMEM((tokens, head), BF16),
            pltpu.VMEM((tokens, head), BF16),
            pltpu.VMEM((n, CAP * unit, head), BF16),
            pltpu.VMEM((n, CAP * unit, head), BF16),
            pltpu.VMEM((n, rows, head), BF16),
            pltpu.VMEM((part, head), F32),
            pltpu.VMEM((part, head), BF16),
            pltpu.VMEM((nf, quarter, head), BF16),
            pltpu.VMEM((nf, quarter, head), BF16),
            dma((4,)),
            dma((blocks,)),
            dma((n,)),
            dma((n,)),
            dma((n,)),
            dma((n,)),
            dma((n,)),
            dma((n,)),
            dma((n,)),
            dma((n,)),
            dma((n,)),
            dma((n,)),
            dma((nf,)),
            dma((nf,)),
            dma((nf,)),
            dma((nf,)),
        ],
        compiler_params=pltpu.CompilerParams(
            collective_id=0, has_side_effects=True, vmem_limit_bytes=48 * 1024 * 1024
        ),
    )(
        owners,
        unit_slots,
        camera,
        pool_weights.reshape(blocks * refs * unit, lbr),
        student,
        head_weight,
    )
    if not fused:
        grad_head = lax.psum(grad_head, "frame")
    return (grad_student, grad_head)


def solution(mesh):
    return jax.shard_map(
        on_device,
        mesh=mesh,
        in_specs=(
            P(("frame", "sector"), None),
            P(("frame", "sector")),
            P(("frame", "sector"), None),
            P(("frame", "sector"), None, None, None),
            P(("frame", "sector"), None),
            P(),
        ),
        out_specs=(P(("frame", "sector"), None), P("sector", None)),
        check_vma=False,
    )
```

```python
import functools

import jax
import jax.numpy as jnp
from jax import lax
from jax.experimental import pallas as pl
from jax.experimental.pallas import tpu as pltpu
from jax.sharding import PartitionSpec as P

CAP = 2
LOSS_WEIGHT = 8.0
EPSILON = 1e-06
F32 = jnp.float32
BF16 = jnp.bfloat16


def dot(a, b):
    return jnp.dot(a, b, preferred_element_type=F32)


def kernel_body(
    sizes,
    owners,
    slots,
    cam_h,
    pool_h,
    stu_h,
    w_h,
    gs_h,
    gh,
    cam,
    pool,
    stu,
    w,
    send,
    recv,
    camt,
    camg,
    bmat,
    bt,
    gt,
    gsv,
    sg,
    back,
    gall,
    acc,
    give,
    got,
    keep,
    fsend,
    frecv,
    zsend,
    zrecv,
    fgat,
    load_sem,
    store_sem,
    fs,
    fr,
    cs,
    cr,
    bs,
    br,
    gs_sem,
    gr_sem,
    ps,
    pr,
    es,
    er,
    xs,
    xr,
    zs,
    zr,
    ys,
    yr,
):
    n, nf, units, unit, blocks, refs, lbr, fused = sizes
    rows, width = cam.shape
    head = w.shape[1]
    slot_rows = n * CAP * unit
    part = width // n
    me = lax.axis_index("sector")
    mf = lax.axis_index("frame")

    loads = [
        pltpu.make_async_copy(src, dst, load_sem.at[i])
        for i, (src, dst) in enumerate(((cam_h, cam), (w_h, w), (pool_h, pool), (stu_h, stu)))
    ]
    for copy in loads:
        copy.start()

    def remote(src, dst, ssem, rsem, frame, sector):
        return pltpu.make_async_remote_copy(
            src_ref=src,
            dst_ref=dst,
            send_sem=ssem,
            recv_sem=rsem,
            device_id=(frame, sector),
            device_id_type=pl.DeviceIdType.MESH,
        )

    barrier = pltpu.get_barrier_semaphore()
    for i in range(1, n):
        pl.semaphore_signal(
            barrier, inc=1, device_id=(mf, lax.rem(me + i, n)), device_id_type=pl.DeviceIdType.MESH
        )
    greeted = n - 1
    if fused:
        for i in range(1, nf):
            pl.semaphore_signal(
                barrier,
                inc=1,
                device_id=(lax.rem(mf + i, nf), me),
                device_id_type=pl.DeviceIdType.MESH,
            )
        greeted += nf - 1

    dest = []
    for u in range(units):
        rank = jnp.int32(0)
        for v in range(u):
            rank = rank + jnp.where(owners[v] == owners[u], 1, 0).astype(jnp.int32)
        dest.append(owners[u] * CAP + rank)

    column = lax.broadcasted_iota(jnp.int32, (1, rows), 1)
    place_row = lax.rem(column, unit)
    for u in range(units):
        place_row = place_row + jnp.where(column // unit == u, dest[u] * unit, 0)
    place = (
        lax.broadcasted_iota(jnp.int32, (slot_rows, rows), 0) == place_row
    ).astype(F32).astype(BF16)

    loads[0].wait()
    loads[1].wait()
    projected = dot(cam[...], w[...]).astype(BF16)
    placed = dot(place, projected).astype(BF16).reshape(n, CAP * unit, head)
    send[...] = placed
    pl.semaphore_wait(barrier, greeted)
    forward = []
    for i in range(1, n):
        peer = lax.rem(me + i, n)
        copy = remote(send.at[peer], recv.at[me], fs.at[i], fr.at[i], mf, peer)
        copy.start()
        forward.append(copy)
    recv[me] = send[me]

    for i in range(0, width, 128):
        camt[i : i + 128, :] = cam[:, i : i + 128].T
    columns = []
    if not fused:
        for i in range(1, n):
            peer = lax.rem(me + i, n)
            start = pl.multiple_of(peer * part, 16)
            copy = remote(camt.at[pl.ds(start, part)], camg.at[me], cs.at[i], cr.at[i], mf, peer)
            copy.start()
            columns.append(copy)
        camg[me] = camt[pl.ds(pl.multiple_of(me * part, 16), part), :]

    loads[2].wait()
    depth = refs * unit
    ref_column = lax.broadcasted_iota(jnp.int32, (1, depth), 1)
    slot_row = lax.broadcasted_iota(jnp.int32, (slot_rows, depth), 0)
    for b in range(blocks):
        wanted = lax.rem(ref_column, unit)
        for k in range(refs):
            wanted = wanted + jnp.where(ref_column // unit == k, slots[b, k] * unit, 0)
        pick = (slot_row == wanted).astype(F32).astype(BF16)
        combined = dot(pick, pool[b * depth : (b + 1) * depth, :])
        bmat[:, b * lbr : (b + 1) * lbr] = combined.astype(BF16)
        bt[b * lbr : (b + 1) * lbr, :] = combined.T.astype(BF16)

    loads[3].wait()
    for copy in forward:
        copy.wait_recv()
    arrived = recv[...].reshape(slot_rows, head)
    stores = []
    for b in range(blocks):
        span = slice(b * lbr, (b + 1) * lbr)
        target = dot(bt[span, :], arrived)
        learner = stu[span, :].astype(F32)
        inv_t = lax.rsqrt(jnp.sum(target * target, axis=1, keepdims=True) + EPSILON)
        inv_l = lax.rsqrt(jnp.sum(learner * learner, axis=1, keepdims=True) + EPSILON)
        both = inv_t * inv_l
        cosine = jnp.sum(target * learner, axis=1, keepdims=True) * both
        scale = -LOSS_WEIGHT * both
        back_l = LOSS_WEIGHT * cosine * (inv_l * inv_l)
        back_t = LOSS_WEIGHT * cosine * (inv_t * inv_t)
        gsv[span, :] = (target * scale + learner * back_l).astype(BF16)
        gt[span, :] = (learner * scale + target * back_t).astype(BF16)
        store = pltpu.make_async_copy(gsv.at[span], gs_h.at[span], store_sem.at[b])
        store.start()
        stores.append(store)

    sg[...] = dot(bmat[...], gt[...]).astype(BF16).reshape(n, CAP * unit, head)
    returns = []
    for i in range(1, n):
        peer = lax.rem(me + i, n)
        copy = remote(sg.at[peer], back.at[me], bs.at[i], br.at[i], mf, peer)
        copy.start()
        returns.append(copy)
    back[me] = sg[me]

    place_column = lax.broadcasted_iota(jnp.int32, (rows, 1), 0)
    home_row = lax.rem(place_column, unit)
    for u in range(units):
        home_row = home_row + jnp.where(place_column // unit == u, dest[u] * unit, 0)
    home = (
        lax.broadcasted_iota(jnp.int32, (rows, slot_rows), 1) == home_row
    ).astype(F32).astype(BF16)
    for copy in returns:
        copy.wait_recv()
    row_grads = dot(home, back[...].reshape(slot_rows, head)).astype(BF16)
    pending = forward + returns
    nz = n // 2
    z = me // 2
    core = lax.rem(me, 2)
    twin = z * 2 + (1 - core)
    if fused:
        quarter = part // nf
        order = [lax.rem(z + i, nz) for i in range(1, nz)] + [z]

        def term(zz, c):
            start = pl.multiple_of((zz * 2 + c) * part, 16)
            return dot(camt[pl.ds(start, part), :], row_grads)

        swaps = []
        for i, zz in enumerate(order):
            give[i] = term(zz, 1 - core).astype(BF16)
            copy = remote(give.at[i], got.at[i], es.at[i], er.at[i], mf, twin)
            copy.start()
            swaps.append(copy)
        for i, zz in enumerate(order):
            keep[i] = term(zz, core)
        scatters = []
        for i in range(nz):
            swaps[i].wait_recv()
            pair = keep[i] + got[i].astype(F32)
            keep[i] = pair
            fsend[i] = pair.astype(BF16)
            for j in range(1, nf):
                peer = lax.rem(mf + j, nf)
                start = pl.multiple_of(peer * quarter, 16)
                copy = remote(
                    fsend.at[i, pl.ds(start, quarter)],
                    frecv.at[i, j],
                    xs.at[i, j],
                    xr.at[i, j],
                    peer,
                    me,
                )
                copy.start()
                scatters.append(copy)
        climbs = []
        mine = pl.ds(pl.multiple_of(mf * quarter, 16), quarter)
        for i, zz in enumerate(order):
            total = keep[i, mine, :]
            for j in range(1, nf):
                scatters[i * (nf - 1) + j - 1].wait_recv()
                total = total + frecv[i, j].astype(F32)
            if i < nz - 1:
                zsend[i] = total.astype(BF16)
                copy = remote(
                    zsend.at[i], zrecv.at[i], zs.at[i], zr.at[i], mf, zz * 2 + core
                )
                copy.start()
                climbs.append(copy)
        for i, copy in enumerate(climbs):
            copy.wait_recv()
            total = total + zrecv[i].astype(F32)
        fgat[mf] = total.astype(BF16)
        spreads = []
        for j in range(1, nf):
            peer = lax.rem(mf + j, nf)
            copy = remote(fgat.at[mf], fgat.at[mf], ys.at[j], yr.at[j], peer, me)
            copy.start()
            spreads.append(copy)
        for copy in spreads:
            copy.wait_recv()
        for f in range(nf):
            gh[f * quarter : (f + 1) * quarter, :] = fgat[f]
        pending += swaps + scatters + climbs + spreads
    else:
        gall[me] = row_grads
        gathers = [None]
        for i in range(1, nz):
            peer = lax.rem(z + i, nz) * 2 + core
            copy = remote(gall.at[me], gall.at[me], gs_sem.at[i], gr_sem.at[i], mf, peer)
            copy.start()
            gathers.append(copy)
        passed = [remote(gall.at[me], gall.at[me], ps.at[0], pr.at[0], mf, twin)]
        passed[0].start()
        for copy in columns:
            copy.wait_recv()
        acc[...] = dot(camg[me], gall[me])
        for i in range(1, nz):
            source = lax.rem(z + nz - i, nz) * 2 + core
            gathers[i].wait_recv()
            copy = remote(gall.at[source], gall.at[source], ps.at[i], pr.at[i], mf, twin)
            copy.start()
            passed.append(copy)
            acc[...] += dot(camg[source], gall[source])
        for i in range(nz):
            source = lax.rem(z + nz - i, nz) * 2 + (1 - core)
            passed[i].wait_recv()
            acc[...] += dot(camg[source], gall[source])

        gh[...] = acc[...]
        pending += columns + gathers[1:] + passed
    for copy in pending:
        copy.wait_send()
    for store in stores:
        store.wait()


def on_device(camera, owners, unit_slots, pool_weights, student, head_weight):
    n = lax.axis_size("sector")
    nf = lax.axis_size("frame")
    units = owners.shape[0]
    rows, width = camera.shape
    unit = rows // units
    head = head_weight.shape[1]
    blocks, refs = unit_slots.shape
    lbr = pool_weights.shape[3]
    tokens = blocks * lbr
    slot_rows = n * CAP * unit
    part = width // n
    fused = part % (nf * 16) == 0
    quarter = part // nf if fused else 16
    nz = n // 2 if fused else 1

    def tall(size):
        return 1 if fused else size

    sizes = (n, nf, units, unit, blocks, refs, lbr, fused)
    any_space = pl.BlockSpec(memory_space=pltpu.HBM)
    smem = pl.BlockSpec(memory_space=pltpu.SMEM)
    dma = pltpu.SemaphoreType.DMA
    grad_student, grad_head = pl.pallas_call(
        functools.partial(kernel_body, sizes),
        out_shape=(
            jax.ShapeDtypeStruct((tokens, head), BF16),
            jax.ShapeDtypeStruct((part, head), BF16 if fused else F32),
        ),
        in_specs=[smem, smem, any_space, any_space, any_space, any_space],
        out_specs=(any_space, pl.BlockSpec(memory_space=pltpu.VMEM)),
        scratch_shapes=[
            pltpu.VMEM((rows, width), BF16),
            pltpu.VMEM((blocks * refs * unit, lbr), BF16),
            pltpu.VMEM((tokens, head), BF16),
            pltpu.VMEM((width, head), BF16),
            pltpu.VMEM((n, CAP * unit, head), BF16),
            pltpu.VMEM((n, CAP * unit, head), BF16),
            pltpu.VMEM((width, rows), BF16),
            pltpu.VMEM((tall(n), part, rows), BF16),
            pltpu.VMEM((slot_rows, tokens), BF16),
            pltpu.VMEM((tokens, slot_rows), BF16),
            pltpu.VMEM((tokens, head), BF16),
            pltpu.VMEM((tokens, head), BF16),
            pltpu.VMEM((n, CAP * unit, head), BF16),
            pltpu.VMEM((n, CAP * unit, head), BF16),
            pltpu.VMEM((tall(n), rows, head), BF16),
            pltpu.VMEM((part, head), F32),
            pltpu.VMEM((nz, part, head), BF16),
            pltpu.VMEM((nz, part, head), BF16),
            pltpu.VMEM((nz, part, head), F32),
            pltpu.VMEM((nz, part, head), BF16),
            pltpu.VMEM((nz, nf, quarter, head), BF16),
            pltpu.VMEM((nz, quarter, head), BF16),
            pltpu.VMEM((nz, quarter, head), BF16),
            pltpu.VMEM((nf, quarter, head), BF16),
            dma((4,)),
            dma((blocks,)),
            dma((n,)),
            dma((n,)),
            dma((n,)),
            dma((n,)),
            dma((n,)),
            dma((n,)),
            dma((n,)),
            dma((n,)),
            dma((n,)),
            dma((n,)),
            dma((nz,)),
            dma((nz,)),
            dma((nz, nf)),
            dma((nz, nf)),
            dma((nz,)),
            dma((nz,)),
            dma((nf,)),
            dma((nf,)),
        ],
        compiler_params=pltpu.CompilerParams(
            collective_id=0, has_side_effects=True, vmem_limit_bytes=60 * 1024 * 1024
        ),
    )(
        owners,
        unit_slots,
        camera,
        pool_weights.reshape(blocks * refs * unit, lbr),
        student,
        head_weight,
    )
    if fused:
        grad_head = grad_head.astype(F32)
    else:
        grad_head = lax.psum(grad_head, "frame")
    return (grad_student, grad_head)


def solution(mesh):
    return jax.shard_map(
        on_device,
        mesh=mesh,
        in_specs=(
            P(("frame", "sector"), None),
            P(("frame", "sector")),
            P(("frame", "sector"), None),
            P(("frame", "sector"), None, None, None),
            P(("frame", "sector"), None),
            P(),
        ),
        out_specs=(P(("frame", "sector"), None), P("sector", None)),
        check_vma=False,
    )
```

```python
import functools

import jax
import jax.numpy as jnp
from jax import lax
from jax.experimental import pallas as pl
from jax.experimental.pallas import tpu as pltpu
from jax.sharding import PartitionSpec as P

CAP = 2
LOSS_WEIGHT = 8.0
EPSILON = 1e-06
F32 = jnp.float32
BF16 = jnp.bfloat16


def dot(a, b):
    return jnp.dot(a, b, preferred_element_type=F32)


def kernel_body(
    sizes,
    owners,
    slots,
    cam_h,
    pool_h,
    stu_h,
    w_h,
    gs,
    gh,
    cam,
    pool,
    stu,
    w,
    send,
    recv,
    camt,
    camg,
    bmat,
    bt,
    gt,
    sg,
    back,
    gall,
    acc,
    give,
    got,
    keep,
    fsend,
    frecv,
    zsend,
    zrecv,
    fgat,
    load_sem,
    fs,
    fr,
    cs,
    cr,
    bs,
    br,
    gs_sem,
    gr_sem,
    ps,
    pr,
    es,
    er,
    xs,
    xr,
    zs,
    zr,
    ys,
    yr,
):
    n, nf, units, unit, blocks, refs, lbr, fused = sizes
    rows, width = cam.shape
    head = w.shape[1]
    slot_rows = n * CAP * unit
    part = width // n
    me = lax.axis_index("sector")
    mf = lax.axis_index("frame")

    loads = [
        pltpu.make_async_copy(src, dst, load_sem.at[i])
        for i, (src, dst) in enumerate(((cam_h, cam), (w_h, w), (pool_h, pool), (stu_h, stu)))
    ]
    for copy in loads:
        copy.start()

    def remote(src, dst, ssem, rsem, frame, sector):
        return pltpu.make_async_remote_copy(
            src_ref=src,
            dst_ref=dst,
            send_sem=ssem,
            recv_sem=rsem,
            device_id=(frame, sector),
            device_id_type=pl.DeviceIdType.MESH,
        )

    barrier = pltpu.get_barrier_semaphore()
    for i in range(1, n):
        pl.semaphore_signal(
            barrier, inc=1, device_id=(mf, lax.rem(me + i, n)), device_id_type=pl.DeviceIdType.MESH
        )
    greeted = n - 1
    if fused:
        for i in range(1, nf):
            pl.semaphore_signal(
                barrier,
                inc=1,
                device_id=(lax.rem(mf + i, nf), me),
                device_id_type=pl.DeviceIdType.MESH,
            )
        greeted += nf - 1

    dest = []
    for u in range(units):
        rank = jnp.int32(0)
        for v in range(u):
            rank = rank + jnp.where(owners[v] == owners[u], 1, 0).astype(jnp.int32)
        dest.append(owners[u] * CAP + rank)

    column = lax.broadcasted_iota(jnp.int32, (1, rows), 1)
    place_row = lax.rem(column, unit)
    for u in range(units):
        place_row = place_row + jnp.where(column // unit == u, dest[u] * unit, 0)
    place = (
        lax.broadcasted_iota(jnp.int32, (slot_rows, rows), 0) == place_row
    ).astype(F32).astype(BF16)

    loads[0].wait()
    loads[1].wait()
    projected = dot(cam[...], w[...]).astype(BF16)
    placed = dot(place, projected).astype(BF16).reshape(n, CAP * unit, head)
    send[...] = placed
    pl.semaphore_wait(barrier, greeted)
    forward = []
    for i in range(1, n):
        peer = lax.rem(me + i, n)
        copy = remote(send.at[peer], recv.at[me], fs.at[i], fr.at[i], mf, peer)
        copy.start()
        forward.append(copy)
    recv[me] = send[me]

    for i in range(0, width, 128):
        camt[i : i + 128, :] = cam[:, i : i + 128].T
    columns = []
    if not fused:
        for i in range(1, n):
            peer = lax.rem(me + i, n)
            start = pl.multiple_of(peer * part, 16)
            copy = remote(camt.at[pl.ds(start, part)], camg.at[me], cs.at[i], cr.at[i], mf, peer)
            copy.start()
            columns.append(copy)
        camg[me] = camt[pl.ds(pl.multiple_of(me * part, 16), part), :]

    loads[2].wait()
    depth = refs * unit
    ref_column = lax.broadcasted_iota(jnp.int32, (1, depth), 1)
    slot_row = lax.broadcasted_iota(jnp.int32, (slot_rows, depth), 0)
    for b in range(blocks):
        wanted = lax.rem(ref_column, unit)
        for k in range(refs):
            wanted = wanted + jnp.where(ref_column // unit == k, slots[b, k] * unit, 0)
        pick = (slot_row == wanted).astype(F32).astype(BF16)
        combined = dot(pick, pool[b * depth : (b + 1) * depth, :])
        bmat[:, b * lbr : (b + 1) * lbr] = combined.astype(BF16)
        bt[b * lbr : (b + 1) * lbr, :] = combined.T.astype(BF16)

    loads[3].wait()
    for copy in forward:
        copy.wait_recv()
    arrived = recv[...].reshape(slot_rows, head)
    for b in range(blocks):
        span = slice(b * lbr, (b + 1) * lbr)
        target = dot(bt[span, :], arrived)
        learner = stu[span, :].astype(F32)
        inv_t = lax.rsqrt(jnp.sum(target * target, axis=1, keepdims=True) + EPSILON)
        inv_l = lax.rsqrt(jnp.sum(learner * learner, axis=1, keepdims=True) + EPSILON)
        both = inv_t * inv_l
        cosine = jnp.sum(target * learner, axis=1, keepdims=True) * both
        scale = -LOSS_WEIGHT * both
        back_l = LOSS_WEIGHT * cosine * (inv_l * inv_l)
        back_t = LOSS_WEIGHT * cosine * (inv_t * inv_t)
        gs[span, :] = (target * scale + learner * back_l).astype(BF16)
        gt[span, :] = (learner * scale + target * back_t).astype(BF16)

    sg[...] = dot(bmat[...], gt[...]).astype(BF16).reshape(n, CAP * unit, head)
    returns = []
    for i in range(1, n):
        peer = lax.rem(me + i, n)
        copy = remote(sg.at[peer], back.at[me], bs.at[i], br.at[i], mf, peer)
        copy.start()
        returns.append(copy)
    back[me] = sg[me]

    place_column = lax.broadcasted_iota(jnp.int32, (rows, 1), 0)
    home_row = lax.rem(place_column, unit)
    for u in range(units):
        home_row = home_row + jnp.where(place_column // unit == u, dest[u] * unit, 0)
    home = (
        lax.broadcasted_iota(jnp.int32, (rows, slot_rows), 1) == home_row
    ).astype(F32).astype(BF16)
    for copy in returns:
        copy.wait_recv()
    row_grads = dot(home, back[...].reshape(slot_rows, head)).astype(BF16)
    pending = forward + returns
    nz = n // 2
    z = me // 2
    core = lax.rem(me, 2)
    twin = z * 2 + (1 - core)
    if fused:
        quarter = part // nf
        order = [lax.rem(z + i, nz) for i in range(1, nz)] + [z]

        def term(zz, c):
            start = pl.multiple_of((zz * 2 + c) * part, 16)
            return dot(camt[pl.ds(start, part), :], row_grads)

        swaps = []
        for i, zz in enumerate(order):
            give[i] = term(zz, 1 - core).astype(BF16)
            copy = remote(give.at[i], got.at[i], es.at[i], er.at[i], mf, twin)
            copy.start()
            swaps.append(copy)
        for i, zz in enumerate(order):
            keep[i] = term(zz, core)
        scatters = []
        for i in range(nz):
            swaps[i].wait_recv()
            pair = keep[i] + got[i].astype(F32)
            keep[i] = pair
            fsend[i] = pair.astype(BF16)
            for j in range(1, nf):
                peer = lax.rem(mf + j, nf)
                start = pl.multiple_of(peer * quarter, 16)
                copy = remote(
                    fsend.at[i, pl.ds(start, quarter)],
                    frecv.at[i, j],
                    xs.at[i, j],
                    xr.at[i, j],
                    peer,
                    me,
                )
                copy.start()
                scatters.append(copy)
        climbs = []
        mine = pl.ds(pl.multiple_of(mf * quarter, 16), quarter)
        for i, zz in enumerate(order):
            total = keep[i, mine, :]
            for j in range(1, nf):
                scatters[i * (nf - 1) + j - 1].wait_recv()
                total = total + frecv[i, j].astype(F32)
            if i < nz - 1:
                zsend[i] = total.astype(BF16)
                copy = remote(
                    zsend.at[i], zrecv.at[i], zs.at[i], zr.at[i], mf, zz * 2 + core
                )
                copy.start()
                climbs.append(copy)
        for i, copy in enumerate(climbs):
            copy.wait_recv()
            total = total + zrecv[i].astype(F32)
        fgat[mf] = total.astype(BF16)
        spreads = []
        for j in range(1, nf):
            peer = lax.rem(mf + j, nf)
            copy = remote(fgat.at[mf], fgat.at[mf], ys.at[j], yr.at[j], peer, me)
            copy.start()
            spreads.append(copy)
        for copy in spreads:
            copy.wait_recv()
        for f in range(nf):
            gh[f * quarter : (f + 1) * quarter, :] = fgat[f]
        pending += swaps + scatters + climbs + spreads
    else:
        gall[me] = row_grads
        gathers = [None]
        for i in range(1, nz):
            peer = lax.rem(z + i, nz) * 2 + core
            copy = remote(gall.at[me], gall.at[me], gs_sem.at[i], gr_sem.at[i], mf, peer)
            copy.start()
            gathers.append(copy)
        passed = [remote(gall.at[me], gall.at[me], ps.at[0], pr.at[0], mf, twin)]
        passed[0].start()
        for copy in columns:
            copy.wait_recv()
        acc[...] = dot(camg[me], gall[me])
        for i in range(1, nz):
            source = lax.rem(z + nz - i, nz) * 2 + core
            gathers[i].wait_recv()
            copy = remote(gall.at[source], gall.at[source], ps.at[i], pr.at[i], mf, twin)
            copy.start()
            passed.append(copy)
            acc[...] += dot(camg[source], gall[source])
        for i in range(nz):
            source = lax.rem(z + nz - i, nz) * 2 + (1 - core)
            passed[i].wait_recv()
            acc[...] += dot(camg[source], gall[source])

        gh[...] = acc[...]
        pending += columns + gathers[1:] + passed
    for copy in pending:
        copy.wait_send()


def on_device(camera, owners, unit_slots, pool_weights, student, head_weight):
    n = lax.axis_size("sector")
    nf = lax.axis_size("frame")
    units = owners.shape[0]
    rows, width = camera.shape
    unit = rows // units
    head = head_weight.shape[1]
    blocks, refs = unit_slots.shape
    lbr = pool_weights.shape[3]
    tokens = blocks * lbr
    slot_rows = n * CAP * unit
    part = width // n
    fused = part % (nf * 16) == 0
    quarter = part // nf if fused else 16
    nz = n // 2 if fused else 1

    def tall(size):
        return 1 if fused else size

    sizes = (n, nf, units, unit, blocks, refs, lbr, fused)
    any_space = pl.BlockSpec(memory_space=pltpu.HBM)
    smem = pl.BlockSpec(memory_space=pltpu.SMEM)
    dma = pltpu.SemaphoreType.DMA
    grad_student, grad_head = pl.pallas_call(
        functools.partial(kernel_body, sizes),
        out_shape=(
            jax.ShapeDtypeStruct((tokens, head), BF16),
            jax.ShapeDtypeStruct((part, head), BF16 if fused else F32),
        ),
        in_specs=[smem, smem, any_space, any_space, any_space, any_space],
        out_specs=(pl.BlockSpec(memory_space=pltpu.VMEM), pl.BlockSpec(memory_space=pltpu.VMEM)),
        scratch_shapes=[
            pltpu.VMEM((rows, width), BF16),
            pltpu.VMEM((blocks * refs * unit, lbr), BF16),
            pltpu.VMEM((tokens, head), BF16),
            pltpu.VMEM((width, head), BF16),
            pltpu.VMEM((n, CAP * unit, head), BF16),
            pltpu.VMEM((n, CAP * unit, head), BF16),
            pltpu.VMEM((width, rows), BF16),
            pltpu.VMEM((tall(n), part, rows), BF16),
            pltpu.VMEM((slot_rows, tokens), BF16),
            pltpu.VMEM((tokens, slot_rows), BF16),
            pltpu.VMEM((tokens, head), BF16),
            pltpu.VMEM((n, CAP * unit, head), BF16),
            pltpu.VMEM((n, CAP * unit, head), BF16),
            pltpu.VMEM((tall(n), rows, head), BF16),
            pltpu.VMEM((part, head), F32),
            pltpu.VMEM((nz, part, head), BF16),
            pltpu.VMEM((nz, part, head), BF16),
            pltpu.VMEM((nz, part, head), F32),
            pltpu.VMEM((nz, part, head), BF16),
            pltpu.VMEM((nz, nf, quarter, head), BF16),
            pltpu.VMEM((nz, quarter, head), BF16),
            pltpu.VMEM((nz, quarter, head), BF16),
            pltpu.VMEM((nf, quarter, head), BF16),
            dma((4,)),
            dma((n,)),
            dma((n,)),
            dma((n,)),
            dma((n,)),
            dma((n,)),
            dma((n,)),
            dma((n,)),
            dma((n,)),
            dma((n,)),
            dma((n,)),
            dma((nz,)),
            dma((nz,)),
            dma((nz, nf)),
            dma((nz, nf)),
            dma((nz,)),
            dma((nz,)),
            dma((nf,)),
            dma((nf,)),
        ],
        compiler_params=pltpu.CompilerParams(
            collective_id=0, has_side_effects=True, vmem_limit_bytes=40 * 1024 * 1024
        ),
    )(
        *(
            pltpu.with_memory_space_constraint(x, pltpu.HBM)
            for x in (
                owners,
                unit_slots,
                camera,
                pool_weights.reshape(blocks * refs * unit, lbr),
                student,
                head_weight,
            )
        ),
    )
    if fused:
        grad_head = grad_head.astype(F32)
    else:
        grad_head = lax.psum(grad_head, "frame")
    return (grad_student, grad_head)


def solution(mesh):
    return jax.shard_map(
        on_device,
        mesh=mesh,
        in_specs=(
            P(("frame", "sector"), None),
            P(("frame", "sector")),
            P(("frame", "sector"), None),
            P(("frame", "sector"), None, None, None),
            P(("frame", "sector"), None),
            P(),
        ),
        out_specs=(P(("frame", "sector"), None), P("sector", None)),
        check_vma=False,
    )
```

```python
import functools

import jax
import jax.numpy as jnp
from jax import lax
from jax.experimental import pallas as pl
from jax.experimental.pallas import tpu as pltpu
from jax.sharding import PartitionSpec as P

CAP = 2
LOSS_WEIGHT = 8.0
EPSILON = 1e-06
F32 = jnp.float32
BF16 = jnp.bfloat16


def dot(a, b):
    return jnp.dot(a, b, preferred_element_type=F32)


def kernel_body(
    sizes,
    owners_h,
    slots_h,
    cam_h,
    pool_h,
    stu_h,
    w_h,
    gs,
    gh,
    owners,
    slots,
    cam,
    pool,
    stu,
    w,
    send,
    recv,
    camt,
    camg,
    bmat,
    bt,
    gt,
    sg,
    back,
    gall,
    acc,
    give,
    got,
    keep,
    fsend,
    frecv,
    zsend,
    zrecv,
    fgat,
    load_sem,
    fs,
    fr,
    cs,
    cr,
    bs,
    br,
    gs_sem,
    gr_sem,
    ps,
    pr,
    es,
    er,
    xs,
    xr,
    zs,
    zr,
    ys,
    yr,
):
    n, nf, units, unit, blocks, refs, lbr, fused = sizes
    rows, width = cam.shape
    head = w.shape[1]
    slot_rows = n * CAP * unit
    part = width // n
    me = lax.axis_index("sector")
    mf = lax.axis_index("frame")

    def remote(src, dst, ssem, rsem, frame, sector):
        return pltpu.make_async_remote_copy(
            src_ref=src,
            dst_ref=dst,
            send_sem=ssem,
            recv_sem=rsem,
            device_id=(frame, sector),
            device_id_type=pl.DeviceIdType.MESH,
        )

    barrier = pltpu.get_barrier_semaphore()
    for i in range(1, n):
        pl.semaphore_signal(
            barrier, inc=1, device_id=(mf, lax.rem(me + i, n)), device_id_type=pl.DeviceIdType.MESH
        )
    greeted = n - 1
    if fused:
        for i in range(1, nf):
            pl.semaphore_signal(
                barrier,
                inc=1,
                device_id=(lax.rem(mf + i, nf), me),
                device_id_type=pl.DeviceIdType.MESH,
            )
        greeted += nf - 1

    loads = [
        pltpu.make_async_copy(src, dst, load_sem.at[i])
        for i, (src, dst) in enumerate(
            (
                (cam_h, cam),
                (w_h, w),
                (pool_h, pool),
                (stu_h, stu),
                (owners_h, owners),
                (slots_h, slots),
            )
        )
    ]
    for copy in loads[4:] + loads[:4]:
        copy.start()

    loads[4].wait()
    loads[5].wait()
    dest = []
    for u in range(units):
        rank = jnp.int32(0)
        for v in range(u):
            rank = rank + jnp.where(owners[v] == owners[u], 1, 0).astype(jnp.int32)
        dest.append(owners[u] * CAP + rank)

    column = lax.broadcasted_iota(jnp.int32, (1, rows), 1)
    place_row = lax.rem(column, unit)
    for u in range(units):
        place_row = place_row + jnp.where(column // unit == u, dest[u] * unit, 0)
    place = (
        lax.broadcasted_iota(jnp.int32, (slot_rows, rows), 0) == place_row
    ).astype(F32).astype(BF16)

    loads[0].wait()
    loads[1].wait()
    projected = dot(cam[...], w[...]).astype(BF16)
    placed = dot(place, projected).astype(BF16).reshape(n, CAP * unit, head)
    send[...] = placed
    pl.semaphore_wait(barrier, greeted)
    forward = []
    for i in range(1, n):
        peer = lax.rem(me + i, n)
        copy = remote(send.at[peer], recv.at[me], fs.at[i], fr.at[i], mf, peer)
        copy.start()
        forward.append(copy)
    recv[me] = send[me]

    for i in range(0, width, 128):
        camt[i : i + 128, :] = cam[:, i : i + 128].T
    columns = []
    if not fused:
        for i in range(1, n):
            peer = lax.rem(me + i, n)
            start = pl.multiple_of(peer * part, 16)
            copy = remote(camt.at[pl.ds(start, part)], camg.at[me], cs.at[i], cr.at[i], mf, peer)
            copy.start()
            columns.append(copy)
        camg[me] = camt[pl.ds(pl.multiple_of(me * part, 16), part), :]

    loads[2].wait()
    depth = refs * unit
    ref_column = lax.broadcasted_iota(jnp.int32, (1, depth), 1)
    slot_row = lax.broadcasted_iota(jnp.int32, (slot_rows, depth), 0)
    for b in range(blocks):
        wanted = lax.rem(ref_column, unit)
        for k in range(refs):
            wanted = wanted + jnp.where(ref_column // unit == k, slots[b, k] * unit, 0)
        pick = (slot_row == wanted).astype(F32).astype(BF16)
        combined = dot(pick, pool[b * depth : (b + 1) * depth, :])
        bmat[:, b * lbr : (b + 1) * lbr] = combined.astype(BF16)
        bt[b * lbr : (b + 1) * lbr, :] = combined.T.astype(BF16)

    loads[3].wait()
    for copy in forward:
        copy.wait_recv()
    arrived = recv[...].reshape(slot_rows, head)
    for b in range(blocks):
        span = slice(b * lbr, (b + 1) * lbr)
        target = dot(bt[span, :], arrived)
        learner = stu[span, :].astype(F32)
        inv_t = lax.rsqrt(jnp.sum(target * target, axis=1, keepdims=True) + EPSILON)
        inv_l = lax.rsqrt(jnp.sum(learner * learner, axis=1, keepdims=True) + EPSILON)
        both = inv_t * inv_l
        cosine = jnp.sum(target * learner, axis=1, keepdims=True) * both
        scale = -LOSS_WEIGHT * both
        back_l = LOSS_WEIGHT * cosine * (inv_l * inv_l)
        back_t = LOSS_WEIGHT * cosine * (inv_t * inv_t)
        gs[span, :] = (target * scale + learner * back_l).astype(BF16)
        gt[span, :] = (learner * scale + target * back_t).astype(BF16)

    sg[...] = dot(bmat[...], gt[...]).astype(BF16).reshape(n, CAP * unit, head)
    returns = []
    for i in range(1, n):
        peer = lax.rem(me + i, n)
        copy = remote(sg.at[peer], back.at[me], bs.at[i], br.at[i], mf, peer)
        copy.start()
        returns.append(copy)
    back[me] = sg[me]

    place_column = lax.broadcasted_iota(jnp.int32, (rows, 1), 0)
    home_row = lax.rem(place_column, unit)
    for u in range(units):
        home_row = home_row + jnp.where(place_column // unit == u, dest[u] * unit, 0)
    home = (
        lax.broadcasted_iota(jnp.int32, (rows, slot_rows), 1) == home_row
    ).astype(F32).astype(BF16)
    for copy in returns:
        copy.wait_recv()
    row_grads = dot(home, back[...].reshape(slot_rows, head)).astype(BF16)
    pending = forward + returns
    nz = n // 2
    z = me // 2
    core = lax.rem(me, 2)
    twin = z * 2 + (1 - core)
    if fused:
        quarter = part // nf
        order = [lax.rem(z + i, nz) for i in range(1, nz)] + [z]

        def term(zz, c):
            start = pl.multiple_of((zz * 2 + c) * part, 16)
            return dot(camt[pl.ds(start, part), :], row_grads)

        swaps = []
        scatters = []
        for i in range(nz + 1):
            if i < nz:
                give[i] = term(order[i], 1 - core).astype(BF16)
                copy = remote(give.at[i], got.at[i], es.at[i], er.at[i], mf, twin)
                copy.start()
                swaps.append(copy)
            if i == 0:
                continue
            k = i - 1
            kept = term(order[k], core)
            swaps[k].wait_recv()
            pair = kept + got[k].astype(F32)
            fsend[k] = pair.astype(BF16)
            for j in range(1, nf):
                peer = lax.rem(mf + j, nf)
                start = pl.multiple_of(peer * quarter, 16)
                copy = remote(
                    fsend.at[k, pl.ds(start, quarter)],
                    frecv.at[k, j],
                    xs.at[k, j],
                    xr.at[k, j],
                    peer,
                    me,
                )
                copy.start()
                scatters.append(copy)
            keep[k] = pair
        climbs = []
        mine = pl.ds(pl.multiple_of(mf * quarter, 16), quarter)
        for i, zz in enumerate(order):
            total = keep[i, mine, :]
            for j in range(1, nf):
                scatters[i * (nf - 1) + j - 1].wait_recv()
                total = total + frecv[i, j].astype(F32)
            if i < nz - 1:
                zsend[i] = total.astype(BF16)
                copy = remote(
                    zsend.at[i], zrecv.at[i], zs.at[i], zr.at[i], mf, zz * 2 + core
                )
                copy.start()
                climbs.append(copy)
        for i, copy in enumerate(climbs):
            copy.wait_recv()
            total = total + zrecv[i].astype(F32)
        fgat[mf] = total.astype(BF16)
        spreads = []
        for j in range(1, nf):
            peer = lax.rem(mf + j, nf)
            copy = remote(fgat.at[mf], fgat.at[mf], ys.at[j], yr.at[j], peer, me)
            copy.start()
            spreads.append(copy)
        for copy in spreads:
            copy.wait_recv()
        for f in range(nf):
            gh[f * quarter : (f + 1) * quarter, :] = fgat[f]
        pending += swaps + scatters + climbs + spreads
    else:
        gall[me] = row_grads
        gathers = [None]
        for i in range(1, nz):
            peer = lax.rem(z + i, nz) * 2 + core
            copy = remote(gall.at[me], gall.at[me], gs_sem.at[i], gr_sem.at[i], mf, peer)
            copy.start()
            gathers.append(copy)
        passed = [remote(gall.at[me], gall.at[me], ps.at[0], pr.at[0], mf, twin)]
        passed[0].start()
        for copy in columns:
            copy.wait_recv()
        acc[...] = dot(camg[me], gall[me])
        for i in range(1, nz):
            source = lax.rem(z + nz - i, nz) * 2 + core
            gathers[i].wait_recv()
            copy = remote(gall.at[source], gall.at[source], ps.at[i], pr.at[i], mf, twin)
            copy.start()
            passed.append(copy)
            acc[...] += dot(camg[source], gall[source])
        for i in range(nz):
            source = lax.rem(z + nz - i, nz) * 2 + (1 - core)
            passed[i].wait_recv()
            acc[...] += dot(camg[source], gall[source])

        gh[...] = acc[...]
        pending += columns + gathers[1:] + passed
    for copy in pending:
        copy.wait_send()


def on_device(camera, owners, unit_slots, pool_weights, student, head_weight):
    n = lax.axis_size("sector")
    nf = lax.axis_size("frame")
    units = owners.shape[0]
    rows, width = camera.shape
    unit = rows // units
    head = head_weight.shape[1]
    blocks, refs = unit_slots.shape
    lbr = pool_weights.shape[3]
    tokens = blocks * lbr
    slot_rows = n * CAP * unit
    part = width // n
    fused = part % (nf * 16) == 0
    quarter = part // nf if fused else 16
    nz = n // 2 if fused else 1

    def tall(size):
        return 1 if fused else size

    sizes = (n, nf, units, unit, blocks, refs, lbr, fused)
    any_space = pl.BlockSpec(memory_space=pltpu.HBM)
    dma = pltpu.SemaphoreType.DMA
    grad_student, grad_head = pl.pallas_call(
        functools.partial(kernel_body, sizes),
        out_shape=(
            jax.ShapeDtypeStruct((tokens, head), BF16),
            jax.ShapeDtypeStruct((part, head), BF16 if fused else F32),
        ),
        in_specs=[any_space, any_space, any_space, any_space, any_space, any_space],
        out_specs=(pl.BlockSpec(memory_space=pltpu.VMEM), pl.BlockSpec(memory_space=pltpu.VMEM)),
        scratch_shapes=[
            pltpu.SMEM(owners.shape, jnp.int32),
            pltpu.SMEM(unit_slots.shape, jnp.int32),
            pltpu.VMEM((rows, width), BF16),
            pltpu.VMEM((blocks * refs * unit, lbr), BF16),
            pltpu.VMEM((tokens, head), BF16),
            pltpu.VMEM((width, head), BF16),
            pltpu.VMEM((n, CAP * unit, head), BF16),
            pltpu.VMEM((n, CAP * unit, head), BF16),
            pltpu.VMEM((width, rows), BF16),
            pltpu.VMEM((tall(n), part, rows), BF16),
            pltpu.VMEM((slot_rows, tokens), BF16),
            pltpu.VMEM((tokens, slot_rows), BF16),
            pltpu.VMEM((tokens, head), BF16),
            pltpu.VMEM((n, CAP * unit, head), BF16),
            pltpu.VMEM((n, CAP * unit, head), BF16),
            pltpu.VMEM((tall(n), rows, head), BF16),
            pltpu.VMEM((part, head), F32),
            pltpu.VMEM((nz, part, head), BF16),
            pltpu.VMEM((nz, part, head), BF16),
            pltpu.VMEM((nz, part, head), F32),
            pltpu.VMEM((nz, part, head), BF16),
            pltpu.VMEM((nz, nf, quarter, head), BF16),
            pltpu.VMEM((nz, quarter, head), BF16),
            pltpu.VMEM((nz, quarter, head), BF16),
            pltpu.VMEM((nf, quarter, head), BF16),
            dma((6,)),
            dma((n,)),
            dma((n,)),
            dma((n,)),
            dma((n,)),
            dma((n,)),
            dma((n,)),
            dma((n,)),
            dma((n,)),
            dma((n,)),
            dma((n,)),
            dma((nz,)),
            dma((nz,)),
            dma((nz, nf)),
            dma((nz, nf)),
            dma((nz,)),
            dma((nz,)),
            dma((nf,)),
            dma((nf,)),
        ],
        compiler_params=pltpu.CompilerParams(
            collective_id=0, has_side_effects=True, vmem_limit_bytes=40 * 1024 * 1024
        ),
    )(
        *(
            pltpu.with_memory_space_constraint(x, pltpu.HBM)
            for x in (
                owners,
                unit_slots,
                camera,
                pool_weights.reshape(blocks * refs * unit, lbr),
                student,
                head_weight,
            )
        ),
    )
    if fused:
        grad_head = grad_head.astype(F32)
    else:
        grad_head = lax.psum(grad_head, "frame")
    return (grad_student, grad_head)


def solution(mesh):
    return jax.shard_map(
        on_device,
        mesh=mesh,
        in_specs=(
            P(("frame", "sector"), None),
            P(("frame", "sector")),
            P(("frame", "sector"), None),
            P(("frame", "sector"), None, None, None),
            P(("frame", "sector"), None),
            P(),
        ),
        out_specs=(P(("frame", "sector"), None), P("sector", None)),
        check_vma=False,
    )
```

```python
import functools

import jax
import jax.numpy as jnp
from jax import lax
from jax.experimental import pallas as pl
from jax.experimental.pallas import tpu as pltpu
from jax.sharding import PartitionSpec as P

CAP = 2
LOSS_WEIGHT = 8.0
EPSILON = 1e-06
F32 = jnp.float32
BF16 = jnp.bfloat16


def dot(a, b):
    return jnp.dot(a, b, preferred_element_type=F32)


def kernel_body(
    sizes,
    owners_h,
    slots_h,
    cam_h,
    pool_h,
    stu_h,
    w_h,
    gs,
    gh,
    owners,
    slots,
    cam,
    pool,
    stu,
    w,
    send,
    recv,
    camt,
    camg,
    bmat,
    bt,
    gt,
    sg,
    back,
    gall,
    acc,
    give,
    got,
    keep,
    fsend,
    frecv,
    zsend,
    zrecv,
    fgat,
    load_sem,
    fs,
    fr,
    cs,
    cr,
    bs,
    br,
    gs_sem,
    gr_sem,
    ps,
    pr,
    es,
    er,
    xs,
    xr,
    zs,
    zr,
    ys,
    yr,
):
    n, nf, units, unit, blocks, refs, lbr, fused = sizes
    rows, width = cam.shape
    head = w.shape[1]
    slot_rows = n * CAP * unit
    part = width // n
    me = lax.axis_index("sector")
    mf = lax.axis_index("frame")

    def remote(src, dst, ssem, rsem, frame, sector):
        return pltpu.make_async_remote_copy(
            src_ref=src,
            dst_ref=dst,
            send_sem=ssem,
            recv_sem=rsem,
            device_id=(frame, sector),
            device_id_type=pl.DeviceIdType.MESH,
        )

    barrier = pltpu.get_barrier_semaphore()
    for i in range(1, n):
        pl.semaphore_signal(
            barrier, inc=1, device_id=(mf, lax.rem(me + i, n)), device_id_type=pl.DeviceIdType.MESH
        )
    greeted = n - 1
    if fused:
        for i in range(1, nf):
            pl.semaphore_signal(
                barrier,
                inc=1,
                device_id=(lax.rem(mf + i, nf), me),
                device_id_type=pl.DeviceIdType.MESH,
            )
        greeted += nf - 1

    loads = [
        pltpu.make_async_copy(src, dst, load_sem.at[i])
        for i, (src, dst) in enumerate(
            (
                (cam_h, cam),
                (w_h, w),
                (pool_h, pool),
                (stu_h, stu),
                (owners_h, owners),
                (slots_h, slots),
            )
        )
    ]
    for copy in loads[4:] + loads[:4]:
        copy.start()

    loads[4].wait()
    loads[5].wait()
    dest = []
    for u in range(units):
        rank = jnp.int32(0)
        for v in range(u):
            rank = rank + jnp.where(owners[v] == owners[u], 1, 0).astype(jnp.int32)
        dest.append(owners[u] * CAP + rank)

    column = lax.broadcasted_iota(jnp.int32, (1, rows), 1)
    place_row = lax.rem(column, unit)
    for u in range(units):
        place_row = place_row + jnp.where(column // unit == u, dest[u] * unit, 0)
    place = (
        lax.broadcasted_iota(jnp.int32, (slot_rows, rows), 0) == place_row
    ).astype(F32).astype(BF16)

    loads[0].wait()
    loads[1].wait()
    projected = dot(cam[...], w[...]).astype(BF16)
    placed = dot(place, projected).astype(BF16).reshape(n, CAP * unit, head)
    send[...] = placed
    pl.semaphore_wait(barrier, greeted)
    forward = []
    for i in range(1, n):
        peer = lax.rem(me + i, n)
        copy = remote(send.at[peer], recv.at[me], fs.at[i], fr.at[i], mf, peer)
        copy.start()
        forward.append(copy)
    recv[me] = send[me]

    for i in range(0, width, 128):
        camt[i : i + 128, :] = cam[:, i : i + 128].T
    columns = []
    if not fused:
        for i in range(1, n):
            peer = lax.rem(me + i, n)
            start = pl.multiple_of(peer * part, 16)
            copy = remote(camt.at[pl.ds(start, part)], camg.at[me], cs.at[i], cr.at[i], mf, peer)
            copy.start()
            columns.append(copy)
        camg[me] = camt[pl.ds(pl.multiple_of(me * part, 16), part), :]

    loads[2].wait()
    depth = refs * unit
    ref_column = lax.broadcasted_iota(jnp.int32, (1, depth), 1)
    slot_row = lax.broadcasted_iota(jnp.int32, (slot_rows, depth), 0)
    for b in range(blocks):
        wanted = lax.rem(ref_column, unit)
        for k in range(refs):
            wanted = wanted + jnp.where(ref_column // unit == k, slots[b, k] * unit, 0)
        pick = (slot_row == wanted).astype(F32).astype(BF16)
        combined = dot(pick, pool[b * depth : (b + 1) * depth, :])
        bmat[:, b * lbr : (b + 1) * lbr] = combined.astype(BF16)
        bt[b * lbr : (b + 1) * lbr, :] = combined.T.astype(BF16)

    loads[3].wait()
    for copy in forward:
        copy.wait_recv()
    arrived = recv[...].reshape(slot_rows, head)
    scales = []
    for b in range(blocks):
        span = slice(b * lbr, (b + 1) * lbr)
        target = dot(bt[span, :], arrived)
        learner = stu[span, :].astype(F32)
        inv_t = lax.rsqrt(jnp.sum(target * target, axis=1, keepdims=True) + EPSILON)
        inv_l = lax.rsqrt(jnp.sum(learner * learner, axis=1, keepdims=True) + EPSILON)
        both = inv_t * inv_l
        cosine = jnp.sum(target * learner, axis=1, keepdims=True) * both
        scale = -LOSS_WEIGHT * both
        back_l = LOSS_WEIGHT * cosine * (inv_l * inv_l)
        back_t = LOSS_WEIGHT * cosine * (inv_t * inv_t)
        scales.append((scale, back_l))
        gt[span, :] = (learner * scale + target * back_t).astype(BF16)

    sg[...] = dot(bmat[...], gt[...]).astype(BF16).reshape(n, CAP * unit, head)
    returns = []
    for i in range(1, n):
        peer = lax.rem(me + i, n)
        copy = remote(sg.at[peer], back.at[me], bs.at[i], br.at[i], mf, peer)
        copy.start()
        returns.append(copy)
    back[me] = sg[me]
    for b in range(blocks):
        span = slice(b * lbr, (b + 1) * lbr)
        scale, back_l = scales[b]
        target = dot(bt[span, :], recv[...].reshape(slot_rows, head))
        gs[span, :] = (target * scale + stu[span, :].astype(F32) * back_l).astype(BF16)

    place_column = lax.broadcasted_iota(jnp.int32, (rows, 1), 0)
    home_row = lax.rem(place_column, unit)
    for u in range(units):
        home_row = home_row + jnp.where(place_column // unit == u, dest[u] * unit, 0)
    home = (
        lax.broadcasted_iota(jnp.int32, (rows, slot_rows), 1) == home_row
    ).astype(F32).astype(BF16)
    for copy in returns:
        copy.wait_recv()
    row_grads = dot(home, back[...].reshape(slot_rows, head)).astype(BF16)
    pending = forward + returns
    nz = n // 2
    z = me // 2
    core = lax.rem(me, 2)
    twin = z * 2 + (1 - core)
    if fused:
        quarter = part // nf
        order = [lax.rem(z + i, nz) for i in range(1, nz)] + [z]

        def term(zz, c):
            start = pl.multiple_of((zz * 2 + c) * part, 16)
            return dot(camt[pl.ds(start, part), :], row_grads)

        swaps = []
        scatters = []
        for i in range(nz + 1):
            if i < nz:
                give[i] = term(order[i], 1 - core).astype(BF16)
                copy = remote(give.at[i], got.at[i], es.at[i], er.at[i], mf, twin)
                copy.start()
                swaps.append(copy)
            if i == 0:
                continue
            k = i - 1
            kept = term(order[k], core)
            swaps[k].wait_recv()
            pair = kept + got[k].astype(F32)
            fsend[k] = pair.astype(BF16)
            for j in range(1, nf):
                peer = lax.rem(mf + j, nf)
                start = pl.multiple_of(peer * quarter, 16)
                copy = remote(
                    fsend.at[k, pl.ds(start, quarter)],
                    frecv.at[k, j],
                    xs.at[k, j],
                    xr.at[k, j],
                    peer,
                    me,
                )
                copy.start()
                scatters.append(copy)
            keep[k] = pair
        climbs = []
        mine = pl.ds(pl.multiple_of(mf * quarter, 16), quarter)
        for i, zz in enumerate(order):
            total = keep[i, mine, :]
            for j in range(1, nf):
                scatters[i * (nf - 1) + j - 1].wait_recv()
                total = total + frecv[i, j].astype(F32)
            if i < nz - 1:
                zsend[i] = total.astype(BF16)
                copy = remote(
                    zsend.at[i], zrecv.at[i], zs.at[i], zr.at[i], mf, zz * 2 + core
                )
                copy.start()
                climbs.append(copy)
        for i, copy in enumerate(climbs):
            copy.wait_recv()
            total = total + zrecv[i].astype(F32)
        fgat[mf] = total.astype(BF16)
        spreads = []
        for j in range(1, nf):
            peer = lax.rem(mf + j, nf)
            copy = remote(fgat.at[mf], fgat.at[mf], ys.at[j], yr.at[j], peer, me)
            copy.start()
            spreads.append(copy)
        for copy in spreads:
            copy.wait_recv()
        for f in range(nf):
            gh[f * quarter : (f + 1) * quarter, :] = fgat[f]
        pending += swaps + scatters + climbs + spreads
    else:
        gall[me] = row_grads
        gathers = [None]
        for i in range(1, nz):
            peer = lax.rem(z + i, nz) * 2 + core
            copy = remote(gall.at[me], gall.at[me], gs_sem.at[i], gr_sem.at[i], mf, peer)
            copy.start()
            gathers.append(copy)
        passed = [remote(gall.at[me], gall.at[me], ps.at[0], pr.at[0], mf, twin)]
        passed[0].start()
        for copy in columns:
            copy.wait_recv()
        acc[...] = dot(camg[me], gall[me])
        for i in range(1, nz):
            source = lax.rem(z + nz - i, nz) * 2 + core
            gathers[i].wait_recv()
            copy = remote(gall.at[source], gall.at[source], ps.at[i], pr.at[i], mf, twin)
            copy.start()
            passed.append(copy)
            acc[...] += dot(camg[source], gall[source])
        for i in range(nz):
            source = lax.rem(z + nz - i, nz) * 2 + (1 - core)
            passed[i].wait_recv()
            acc[...] += dot(camg[source], gall[source])

        gh[...] = acc[...]
        pending += columns + gathers[1:] + passed
    for copy in pending:
        copy.wait_send()


def on_device(camera, owners, unit_slots, pool_weights, student, head_weight):
    n = lax.axis_size("sector")
    nf = lax.axis_size("frame")
    units = owners.shape[0]
    rows, width = camera.shape
    unit = rows // units
    head = head_weight.shape[1]
    blocks, refs = unit_slots.shape
    lbr = pool_weights.shape[3]
    tokens = blocks * lbr
    slot_rows = n * CAP * unit
    part = width // n
    fused = part % (nf * 16) == 0
    quarter = part // nf if fused else 16
    nz = n // 2 if fused else 1

    def tall(size):
        return 1 if fused else size

    sizes = (n, nf, units, unit, blocks, refs, lbr, fused)
    any_space = pl.BlockSpec(memory_space=pltpu.HBM)
    dma = pltpu.SemaphoreType.DMA
    grad_student, grad_head = pl.pallas_call(
        functools.partial(kernel_body, sizes),
        out_shape=(
            jax.ShapeDtypeStruct((tokens, head), BF16),
            jax.ShapeDtypeStruct((part, head), BF16 if fused else F32),
        ),
        in_specs=[any_space, any_space, any_space, any_space, any_space, any_space],
        out_specs=(pl.BlockSpec(memory_space=pltpu.VMEM), pl.BlockSpec(memory_space=pltpu.VMEM)),
        scratch_shapes=[
            pltpu.SMEM(owners.shape, jnp.int32),
            pltpu.SMEM(unit_slots.shape, jnp.int32),
            pltpu.VMEM((rows, width), BF16),
            pltpu.VMEM((blocks * refs * unit, lbr), BF16),
            pltpu.VMEM((tokens, head), BF16),
            pltpu.VMEM((width, head), BF16),
            pltpu.VMEM((n, CAP * unit, head), BF16),
            pltpu.VMEM((n, CAP * unit, head), BF16),
            pltpu.VMEM((width, rows), BF16),
            pltpu.VMEM((tall(n), part, rows), BF16),
            pltpu.VMEM((slot_rows, tokens), BF16),
            pltpu.VMEM((tokens, slot_rows), BF16),
            pltpu.VMEM((tokens, head), BF16),
            pltpu.VMEM((n, CAP * unit, head), BF16),
            pltpu.VMEM((n, CAP * unit, head), BF16),
            pltpu.VMEM((tall(n), rows, head), BF16),
            pltpu.VMEM((part, head), F32),
            pltpu.VMEM((nz, part, head), BF16),
            pltpu.VMEM((nz, part, head), BF16),
            pltpu.VMEM((nz, part, head), F32),
            pltpu.VMEM((nz, part, head), BF16),
            pltpu.VMEM((nz, nf, quarter, head), BF16),
            pltpu.VMEM((nz, quarter, head), BF16),
            pltpu.VMEM((nz, quarter, head), BF16),
            pltpu.VMEM((nf, quarter, head), BF16),
            dma((6,)),
            dma((n,)),
            dma((n,)),
            dma((n,)),
            dma((n,)),
            dma((n,)),
            dma((n,)),
            dma((n,)),
            dma((n,)),
            dma((n,)),
            dma((n,)),
            dma((nz,)),
            dma((nz,)),
            dma((nz, nf)),
            dma((nz, nf)),
            dma((nz,)),
            dma((nz,)),
            dma((nf,)),
            dma((nf,)),
        ],
        compiler_params=pltpu.CompilerParams(
            collective_id=0, has_side_effects=True, vmem_limit_bytes=40 * 1024 * 1024
        ),
    )(
        *(
            pltpu.with_memory_space_constraint(x, pltpu.HBM)
            for x in (
                owners,
                unit_slots,
                camera,
                pool_weights.reshape(blocks * refs * unit, lbr),
                student,
                head_weight,
            )
        ),
    )
    if fused:
        grad_head = grad_head.astype(F32)
    else:
        grad_head = lax.psum(grad_head, "frame")
    return (grad_student, grad_head)


def solution(mesh):
    return jax.shard_map(
        on_device,
        mesh=mesh,
        in_specs=(
            P(("frame", "sector"), None),
            P(("frame", "sector")),
            P(("frame", "sector"), None),
            P(("frame", "sector"), None, None, None),
            P(("frame", "sector"), None),
            P(),
        ),
        out_specs=(P(("frame", "sector"), None), P("sector", None)),
        check_vma=False,
    )
```
